256 devices in a mesh: section: 8 (over z), dom: 32 (over y, x, core).
Axes of the slice: x: 4, y: 4, z: 8, core: 2. Of those that a mesh axis runs over, the one named last changes fastest.
Arguments:
- features: bfloat16 [2, 8192, 512], P(None, 'dom', 'section'), may hold values from -6 to 6
- send_ids: int32 [1024, 16], P('dom'), may hold values from 0 to 255
- key_list: int32 [64, 4], P('dom'), may hold values from 0 to 5
- key_count: int32 [64], P('dom'), may hold values from 1 to 4
- norm_gain1: bfloat16 [8, 512], P('section'), may hold values from 0.099609375 to 1.8984375
- w_query: bfloat16 [8, 512, 512], P('section')
- w_key: bfloat16 [8, 512, 512], P('section')
- w_value: bfloat16 [8, 512, 512], P('section'), may hold values from -0.25 to 0.25
- w_out: bfloat16 [8, 512, 512], P('section'), may hold values from -0.25 to 0.25
- norm_gain2: bfloat16 [8, 512], P('section'), may hold values from 0.099609375 to 1.8984375
- w_up: bfloat16 [8, 512, 1024], P('section'), may hold values from -0.25 to 0.25
- w_down: bfloat16 [8, 1024, 512], P('section'), may hold values from -0.1875 to 0.1875
Outputs:
- result: float32 [2, 8192, 512], P(None, 'dom', 'section')
The draws below stay inside these ranges and needn't reach their ends.
Inputs may be any that keep to these rules, and one draw needn't show every extreme that they name: `send_ids`: local node numbers of the sending partition. `key_list`: blocks of the extended keys of the query block's partition: its own 2 blocks, then its received boundary rows in blocks of 128.
All inputs are finite; a program needn't handle non-finite values.
Results may differ from the reference program's by a relative error of at most 0.035.
Values may be sent and summed in bfloat16 or wider, within the bound.
A program may use at most 64 MiB of HBM per device.

```python
import jax
import jax.numpy as jnp
from jax import lax

D = 512
HEADS = 8
FF = 1024
BLOCK = 128
KB = 4
LPS = 1
MB = 2
NODE_DEV = 256
PEER_ROWS = 16
NODES = 8192
NBLK = 64
EXT_BLK = 6
LAYERS = 8
N_SECTION = 8
N_DOM = 32


def draw_key_count(key, part):
    counts = jax.random.randint(jax.random.fold_in(key, 3), (NBLK,), 1, KB + 1, dtype=jnp.int32)
    counts = counts.at[0].set(KB)
    counts = counts.at[NBLK - 1].set(1)
    return counts


def draw_w_query(key, part):
    values = jax.random.normal(jax.random.fold_in(key, 11), (LAYERS, D, D), jnp.float32) * D ** (-0.5)
    return values.astype(jnp.bfloat16)


def draw_w_key(key, part):
    values = jax.random.normal(jax.random.fold_in(key, 17), (LAYERS, D, D), jnp.float32) * D ** (-0.5)
    return values.astype(jnp.bfloat16)


def plant(array, rng, smallest, largest):
    longest = array.shape.index(max(array.shape))
    spots = []
    for shift in (0, 1):
        where = [jax.random.randint(jax.random.fold_in(rng, axis), (), 0, length) for axis, length in enumerate(array.shape)]
        where[longest] = (where[longest] + shift) % array.shape[longest]
        spots.append(tuple(where))
    return array.at[spots[0]].set(smallest).at[spots[1]].set(largest)


def shard_levels(key, shape, shards, smallest, top_value):
    level, own = 1.0, jax.random.fold_in(key, 6)
    for position, parts in shards:
        draws = jnp.exp(jax.random.uniform(jax.random.fold_in(own, position), (parts,), jnp.float32, smallest / len(shards), top_value / len(shards)))
        level = level * jnp.repeat(draws, shape[position] // parts).reshape([-1 if axis == position else 1 for axis in range(len(shape))])
    return level


def scatter_about(rng, dims, spread, bound, split=(), kind=jnp.bfloat16):
    values = spread * jax.random.normal(rng, dims, jnp.float32)
    if split:
        values = values * shard_levels(rng, dims, split, -0.22, 0.18)
    return jnp.clip(values, -bound, bound).astype(kind)


def setup_inputs(seed: int = 0) -> dict:
    key_of = jax.random.split(jax.random.key(seed), 13)
    return {
        "features": scatter_about(key_of[0], (MB, NODES, D), 1.0, 6.0, ((1, 32), (2, 8))),
        "send_ids": plant(jax.random.randint(key_of[1], (N_DOM * N_DOM, PEER_ROWS), 0, NODE_DEV), jax.random.fold_in(key_of[1], 1), 0, NODE_DEV - 1).astype(jnp.int32),
        "key_list": plant(jax.random.randint(key_of[2], (NBLK, KB), 0, EXT_BLK), jax.random.fold_in(key_of[2], 1), 0, EXT_BLK - 1).astype(jnp.int32),
        "key_count": draw_key_count(jax.random.fold_in(key_of[12], 71), 0),
        "norm_gain1": jnp.clip(1.0 + 0.18 * jax.random.normal(key_of[4], (LAYERS, D), jnp.float32), 0.099609375, 1.8984375).astype(jnp.bfloat16),
        "w_query": draw_w_query(jax.random.fold_in(key_of[12], 71), 0),
        "w_key": draw_w_key(jax.random.fold_in(key_of[12], 71), 0),
        "w_value": scatter_about(key_of[7], (LAYERS, D, D), D ** -0.5, 0.25, ((0, 8),)),
        "w_out": scatter_about(key_of[8], (LAYERS, D, D), D ** -0.5, 0.25, ((0, 8),)),
        "norm_gain2": jnp.clip(1.0 + 0.18 * jax.random.normal(key_of[9], (LAYERS, D), jnp.float32), 0.099609375, 1.8984375).astype(jnp.bfloat16),
        "w_up": scatter_about(key_of[10], (LAYERS, D, FF), D ** -0.5, 0.25, ((0, 8),)),
        "w_down": scatter_about(key_of[11], (LAYERS, FF, D), FF ** -0.5, 0.1875, ((0, 8),)),
    }


epsilon = 1e-05

def layer_norm(values, gain):
    mean_value = lax.optimization_barrier(jnp.mean(values, axis=-1, keepdims=True))
    centred = values - mean_value
    variance = lax.optimization_barrier(jnp.mean(centred * centred, axis=-1, keepdims=True))
    return centred * lax.rsqrt(variance + epsilon) * gain.astype(jnp.float32)

def math_sqrt(number):
    return float(number) ** 0.5

def block_attention(queries, keys_ext, values_ext, key_slots, slot_count):
    blocks = queries.shape[0] // BLOCK
    head_size = queries.shape[1] // HEADS
    own_block = jnp.arange(blocks, dtype=jnp.int32)[:, None]
    chosen = jnp.concatenate([own_block, key_slots.astype(jnp.int32)], axis=1)
    slots = chosen.shape[1]
    key_rows = keys_ext[chosen].reshape(blocks, slots * BLOCK, HEADS, head_size)
    value_rows = values_ext[chosen].reshape(blocks, slots * BLOCK, HEADS, head_size)
    query_rows = queries.reshape(blocks, BLOCK, HEADS, head_size)
    scores = jnp.einsum('bqhd,bkhd->bhqk', query_rows.astype(jnp.float32), key_rows.astype(jnp.float32))
    scores = scores * (1.0 / math_sqrt(head_size))
    live = jnp.arange(slots, dtype=jnp.int32)[None, :] <= slot_count.astype(jnp.int32)[:, None]
    live_keys = jnp.repeat(live, BLOCK, axis=1)
    scores = jnp.where(live_keys[:, None, None, :], scores, -1e+30)
    highest = lax.optimization_barrier(jnp.max(scores, axis=-1, keepdims=True))
    weights = jnp.exp(scores - highest)
    total = lax.optimization_barrier(jnp.sum(weights, axis=-1, keepdims=True))
    probs = (weights / total).astype(jnp.bfloat16)
    mixed = jnp.einsum('bhqk,bkhd->bqhd', probs.astype(jnp.float32), value_rows.astype(jnp.float32))
    return mixed.reshape(blocks * BLOCK, HEADS * head_size).astype(jnp.bfloat16)

def finish_layer(state, attended, out_weight, gain_two, up_weight, down_weight):
    after = state + jnp.dot(attended, out_weight, preferred_element_type=jnp.float32)
    normed_two = layer_norm(after, gain_two).astype(jnp.bfloat16)
    hidden = jax.nn.gelu(jnp.dot(normed_two, up_weight, preferred_element_type=jnp.float32), approximate=False)
    hidden = hidden.astype(jnp.bfloat16)
    return after + jnp.dot(hidden, down_weight, preferred_element_type=jnp.float32)

def transformer_layer(state, layer_index, send_ids, key_list, key_count, norm_gain1, w_query, w_key, w_value, w_out, norm_gain2, w_up, w_down):
    nodes = state.shape[0]
    width = state.shape[1]
    partitions = nodes // NODE_DEV
    normed = layer_norm(state, norm_gain1[layer_index]).astype(jnp.bfloat16)
    queries = jnp.dot(normed, w_query[layer_index], preferred_element_type=jnp.float32).astype(jnp.bfloat16)
    keys_all = jnp.dot(normed, w_key[layer_index], preferred_element_type=jnp.float32).astype(jnp.bfloat16)
    values_all = jnp.dot(normed, w_value[layer_index], preferred_element_type=jnp.float32).astype(jnp.bfloat16)
    routes = send_ids.astype(jnp.int32).reshape(partitions, partitions, PEER_ROWS)
    source = jnp.arange(partitions, dtype=jnp.int32)[:, None, None]

    def extend(table):
        local_rows = table.reshape(partitions, NODE_DEV, width)
        picked = local_rows[source, routes]
        boundary = jnp.transpose(picked, (1, 0, 2, 3)).reshape(partitions, partitions * PEER_ROWS, width)
        return jnp.concatenate([local_rows, boundary], axis=1).reshape(partitions, -1, BLOCK, width)
    keys_ext = extend(keys_all)
    values_ext = extend(values_all)
    blocks_dev = NODE_DEV // BLOCK
    attended = lax.map(lambda item: block_attention(item[0], item[1], item[2], item[3], item[4]), (queries.reshape(partitions, NODE_DEV, width), keys_ext, values_ext, key_list.reshape(partitions, blocks_dev, KB), key_count.reshape(partitions, blocks_dev)))
    attended = attended.reshape(nodes, width)
    return finish_layer(state, attended, w_out[layer_index], norm_gain2[layer_index], w_up[layer_index], w_down[layer_index])

def reference(features, send_ids, key_list, key_count, norm_gain1, w_query, w_key, w_value, w_out, norm_gain2, w_up, w_down):
    results = []
    for micro_index in range(MB):
        state = features[micro_index].astype(jnp.float32)
        for layer_index in range(N_SECTION * LPS):
            state = transformer_layer(state, layer_index, send_ids, key_list, key_count, norm_gain1, w_query, w_key, w_value, w_out, norm_gain2, w_up, w_down)
        results.append(state)
    return jnp.stack(results)
```

```python
import functools
import math

import jax
import jax.numpy as jnp
from jax import lax
from jax.experimental import pallas as pl
from jax.experimental.pallas import tpu as pltpu
from jax.sharding import PartitionSpec as P

MESH = pl.DeviceIdType.MESH
F32 = jnp.float32
BF16 = jnp.bfloat16

HEADS = 8
BLOCK = 128
MB = 2
PEER = 16
EPS = 1e-05
LOG2 = [0.0, 1.0, math.log2(3.0), 2.0, math.log2(5.0)]
HI = [float(jnp.bfloat16(v)) for v in LOG2]
LO = [v - h for v, h in zip(LOG2, HI)]
DEAD = -1e30


def layer_norm(x, gain):
    mean = jnp.mean(x, axis=-1, keepdims=True)
    centred = x - mean
    var = jnp.mean(centred * centred, axis=-1, keepdims=True)
    return (centred * lax.rsqrt(var + EPS) * gain).astype(BF16)


def mm(a, b):
    return jnp.dot(a, b, preferred_element_type=F32)


def kernel(
    S, N,
    feats, ids, klist, kcount, g1, g2, wq_h, wk_h, wv_h, wo_h, wu_h, wd_h,
    out,
    wq, wk, wv, wo, wu, wd,
    oh, fpack, frecv, hop, hopsend, gsend, halo, kext, vext, att, finsend, finrecv,
    wsem, fs_sem, fr_sem, hs_sem, hr_sem, as_sem, ar_sem, ns_sem, nr_sem,
):
    sec = lax.axis_index("section")
    me = lax.axis_index("dom")
    rows = feats.shape[1]
    half = rows // 2
    cols = feats.shape[2]
    width = cols * S
    halo_rows = N * PEER
    ext = rows + halo_rows
    pairs = HEADS // 2
    blocks = rows // BLOCK
    next_blocks = ext // BLOCK

    barrier = pltpu.get_barrier_semaphore()

    @pl.loop(1, N)
    def _(k):
        pl.semaphore_signal(barrier, inc=1, device_id={"dom": lax.rem(me + k, N)}, device_id_type=MESH)

    @pl.loop(1, S)
    def _(k):
        pl.semaphore_signal(barrier, inc=1, device_id={"section": lax.rem(sec + k, S)}, device_id_type=MESH)

    weights = [
        pltpu.make_async_copy(h.at[0], v, wsem.at[i])
        for i, (h, v) in enumerate(((wq_h, wq), (wk_h, wk), (wv_h, wv), (wo_h, wo), (wu_h, wu), (wd_h, wd)))
    ]
    for w in weights:
        w.start()

    for m in range(MB):
        fpack[m] = jnp.concatenate([feats[m, :half, :], feats[m, half:, :]], axis=1)

    pl.semaphore_wait(barrier, N - 1 + S - 1)

    def feature_copy(m, source):
        return pltpu.make_async_remote_copy(
            src_ref=fpack.at[m], dst_ref=frecv.at[m, source],
            send_sem=fs_sem.at[m], recv_sem=fr_sem.at[m, source],
            device_id={"section": 0}, device_id_type=MESH,
        )

    @pl.when(sec != 0)
    def _():
        for m in range(MB):
            feature_copy(m, sec).start()

    spread = (
        lax.broadcasted_iota(jnp.int32, (halo_rows, N), 0) // PEER
        == lax.broadcasted_iota(jnp.int32, (halo_rows, N), 1)
    ).astype(BF16)
    of_peer = mm(spread, ids[...].astype(F32).astype(BF16))
    picked = jnp.where(
        lax.broadcasted_iota(jnp.int32, (halo_rows, PEER), 0) % PEER
        == lax.broadcasted_iota(jnp.int32, (halo_rows, PEER), 1),
        of_peer,
        0.0,
    )
    id_column = jnp.sum(picked, axis=1, keepdims=True).astype(jnp.int32)
    oh[...] = (id_column == lax.broadcasted_iota(jnp.int32, (halo_rows, rows), 1)).astype(F32).astype(BF16)

    lane = lax.broadcasted_iota(jnp.int32, (BLOCK, 128), 1)
    for e in range(next_blocks):
        tile = jnp.zeros((BLOCK, 128), F32)
        for b in range(blocks):
            times = jnp.int32(1 if e == b else 0)
            for j in range(klist.shape[1]):
                hit = jnp.logical_and(klist[b, j] == e, kcount[b] >= j + 1)
                times = times + jnp.where(hit, 1, 0)
            high = jnp.float32(DEAD)
            low = jnp.float32(0.0)
            for t in range(len(LOG2)):
                high = jnp.where(times == t + 1, jnp.float32(HI[t]), high)
                low = jnp.where(times == t + 1, jnp.float32(LO[t]), low)
            tile = jnp.where(lane == 2 * b, high, tile)
            tile = jnp.where(lane == 2 * b + 1, low, tile)
        for j in range(pairs):
            kext[j, e * BLOCK:(e + 1) * BLOCK, 128:] = tile.astype(BF16)
    for j in range(pairs):
        vext[j, :, 128:] = jnp.ones((ext, 128), BF16)

    gain1 = g1[...].astype(F32)
    gain2 = g2[...].astype(F32)

    def peer_copy(m, target, source):
        return pltpu.make_async_remote_copy(
            src_ref=gsend.at[m, pl.ds(target * PEER, PEER)],
            dst_ref=halo.at[m, pl.ds(source * PEER, PEER)],
            send_sem=as_sem.at[m, target], recv_sem=ar_sem.at[m, source],
            device_id={"dom": target}, device_id_type=MESH,
        )

    def hop_copy(m, target):
        return pltpu.make_async_remote_copy(
            src_ref=hopsend.at[m], dst_ref=hop.at[m],
            send_sem=hs_sem.at[m], recv_sem=hr_sem.at[m],
            device_id={"section": target}, device_id_type=MESH,
        )

    def final_copy(m, target):
        return pltpu.make_async_remote_copy(
            src_ref=finsend.at[m, target], dst_ref=finrecv.at[m],
            send_sem=ns_sem.at[m, target], recv_sem=nr_sem.at[m],
            device_id={"section": target}, device_id_type=MESH,
        )

    qscale = (1.0 / float(width // HEADS) ** 0.5) * math.log2(math.e)
    row_block = lax.broadcasted_iota(jnp.int32, (BLOCK, 128), 1)

    def layer(m):
        @pl.when(sec == 0)
        def _():
            frecv[m, 0] = fpack[m]
            for t in range(1, S):
                feature_copy(m, t).wait_recv()
            for t in range(S // 2):
                a = frecv[m, 2 * t]
                b = frecv[m, 2 * t + 1]
                span = slice(2 * t * cols, 2 * (t + 1) * cols)
                hop[m, :half, span] = jnp.concatenate([a[:, :cols], b[:, :cols]], axis=1)
                hop[m, half:, span] = jnp.concatenate([a[:, cols:], b[:, cols:]], axis=1)

        @pl.when(sec != 0)
        def _():
            hop_copy(m, sec).wait_recv()

        x = hop[m].astype(F32)
        normed = layer_norm(x, gain1)
        gsend[m] = mm(oh[...], normed).astype(BF16)

        @pl.loop(1, N)
        def _(k):
            peer_copy(m, lax.rem(me + k, N), me).start()

        mine = pl.ds(pl.multiple_of(me * PEER, PEER), PEER)
        halo[m, mine, :] = gsend[m, mine, :]

        @pl.when(m == 0)
        def _():
            for w in weights:
                w.wait()

        queries = (mm(normed, wq[...]) * qscale).astype(BF16)
        keys = mm(normed, wk[...]).astype(BF16)
        values = mm(normed, wv[...]).astype(BF16)
        for j in range(pairs):
            kext[j, :rows, :128] = keys[:, j * 128:(j + 1) * 128]
            vext[j, :rows, :128] = values[:, j * 128:(j + 1) * 128]

        @pl.loop(1, N)
        def _(k):
            peer_copy(m, me, lax.rem(me + N - k, N)).wait_recv()

        incoming = halo[m]
        halo_keys = mm(incoming, wk[...]).astype(BF16)
        halo_values = mm(incoming, wv[...]).astype(BF16)
        for j in range(pairs):
            kext[j, rows:, :128] = halo_keys[:, j * 128:(j + 1) * 128]
            vext[j, rows:, :128] = halo_values[:, j * 128:(j + 1) * 128]

        for b in range(blocks):
            pick = jnp.logical_or(row_block == 2 * b, row_block == 2 * b + 1).astype(F32).astype(BF16)
            for j in range(pairs):
                qp = queries[b * BLOCK:(b + 1) * BLOCK, j * 128:(j + 1) * 128]
                mixed = []
                for side in range(2):
                    own = (row_block < 64) if side == 0 else (row_block >= 64)
                    qm = jnp.where(own, qp, jnp.zeros_like(qp))
                    qe = jnp.concatenate([qm, pick], axis=1)
                    s = lax.dot_general(qe, kext[j], (((1,), (1,)), ((), ())), preferred_element_type=F32)
                    top = jnp.max(s, axis=1, keepdims=True)
                    p = jnp.exp2(s - top).astype(BF16)
                    o = mm(p, vext[j])
                    mixed.append(o[:, :128] / o[:, 128:])
                att[b * BLOCK:(b + 1) * BLOCK, j * 128:(j + 1) * 128] = jnp.where(
                    row_block < 64, mixed[0], mixed[1]
                ).astype(BF16)

        after = x + mm(att[...], wo[...])
        normed_two = layer_norm(after, gain2)
        up = mm(normed_two, wu[...])
        hidden = (0.5 * up * (1.0 + lax.erf(up * (0.5 ** 0.5)))).astype(BF16)
        result = after + mm(hidden, wd[...])

        @pl.when(sec != S - 1)
        def _():
            hopsend[m] = result.astype(BF16)
            hop_copy(m, sec + 1).start()

        @pl.when(sec == S - 1)
        def _():
            final = result.astype(BF16)
            for t in range(S):
                piece = final[:, t * cols:(t + 1) * cols]
                finsend[m, t] = jnp.concatenate([piece[:half], piece[half:]], axis=1)
                if t < S - 1:
                    final_copy(m, t).start()
            finrecv[m] = finsend[m, S - 1]

    @pl.loop(0, MB)
    def _(m):
        layer(m)

    for m in range(MB):
        @pl.when(sec != S - 1)
        def _():
            final_copy(m, sec).wait_recv()

        out[m, :half, :] = finrecv[m, :, :cols].astype(F32)
        out[m, half:, :] = finrecv[m, :, cols:].astype(F32)

    for m in range(MB):
        @pl.when(sec != 0)
        def _():
            feature_copy(m, sec).wait_send()

        @pl.when(sec != S - 1)
        def _():
            hop_copy(m, sec + 1).wait_send()

        @pl.when(sec == S - 1)
        def _():
            for t in range(S - 1):
                final_copy(m, t).wait_send()

        @pl.loop(1, N)
        def _(k):
            peer_copy(m, lax.rem(me + k, N), me).wait_send()


def on_device(S, N, feats, ids, klist, kcount, g1, wq, wk, wv, wo, g2, wu, wd):
    mb, rows, cols = feats.shape
    width = cols * S
    ff = wu.shape[2]
    halo_rows = N * PEER
    ext = rows + halo_rows
    pairs = HEADS // 2
    vmem = pl.BlockSpec(memory_space=pltpu.VMEM)
    smem = pl.BlockSpec(memory_space=pltpu.SMEM)
    hbm = pl.BlockSpec(memory_space=pl.ANY)
    dma = pltpu.SemaphoreType.DMA
    return pl.pallas_call(
        functools.partial(kernel, S, N),
        out_shape=jax.ShapeDtypeStruct((mb, rows, cols), F32),
        in_specs=[vmem, vmem, smem, smem, vmem, vmem] + [hbm] * 6,
        out_specs=vmem,
        scratch_shapes=[
            pltpu.VMEM((width, width), BF16),
            pltpu.VMEM((width, width), BF16),
            pltpu.VMEM((width, width), BF16),
            pltpu.VMEM((width, width), BF16),
            pltpu.VMEM((width, ff), BF16),
            pltpu.VMEM((ff, width), BF16),
            pltpu.VMEM((halo_rows, rows), BF16),
            pltpu.VMEM((mb, rows // 2, 2 * cols), BF16),
            pltpu.VMEM((mb, S, rows // 2, 2 * cols), BF16),
            pltpu.VMEM((mb, rows, width), BF16),
            pltpu.VMEM((mb, rows, width), BF16),
            pltpu.VMEM((mb, halo_rows, width), BF16),
            pltpu.VMEM((mb, halo_rows, width), BF16),
            pltpu.VMEM((pairs, ext, 256), BF16),
            pltpu.VMEM((pairs, ext, 256), BF16),
            pltpu.VMEM((rows, width), BF16),
            pltpu.VMEM((mb, S, rows // 2, 2 * cols), BF16),
            pltpu.VMEM((mb, rows // 2, 2 * cols), BF16),
            dma((6,)),
            dma((mb,)),
            dma((mb, S)),
            dma((mb,)),
            dma((mb,)),
            dma((mb, N)),
            dma((mb, N)),
            dma((mb, S)),
            dma((mb,)),
        ],
        compiler_params=pltpu.CompilerParams(collective_id=0, has_side_effects=True),
    )(feats, ids, klist, kcount, g1, g2, wq, wk, wv, wo, wu, wd)


def solution(mesh):
    return jax.shard_map(
        functools.partial(on_device, mesh.shape["section"], mesh.shape["dom"]),
        mesh=mesh,
        in_specs=(
            P(None, "dom", "section"),
            P("dom", None),
            P("dom", None),
            P("dom"),
            P("section", None),
            P("section", None, None),
            P("section", None, None),
            P("section", None, None),
            P("section", None, None),
            P("section", None),
            P("section", None, None),
            P("section", None, None),
        ),
        out_specs=P(None, "dom", "section"),
        check_vma=False,
    )
```

```python
import functools
import math

import jax
import jax.numpy as jnp
from jax import lax
from jax.experimental import pallas as pl
from jax.experimental.pallas import tpu as pltpu
from jax.sharding import PartitionSpec as P

MESH = pl.DeviceIdType.MESH
F32 = jnp.float32
BF16 = jnp.bfloat16

HEADS = 8
BLOCK = 128
MB = 2
PEER = 16
CHUNKS = 4
EPS = 1e-05
DEAD = -1e30
LOG2 = [0.0, 1.0, math.log2(3.0), 2.0, math.log2(5.0)]


def layer_norm(x, gain):
    mean = jnp.mean(x, axis=-1, keepdims=True)
    centred = x - mean
    var = jnp.mean(centred * centred, axis=-1, keepdims=True)
    return (centred * lax.rsqrt(var + EPS) * gain).astype(BF16)


def mm(a, b):
    return jnp.dot(a, b, preferred_element_type=F32)


def mm_t(a, b):
    return lax.dot_general(a, b, (((1,), (1,)), ((), ())), preferred_element_type=F32)


def far_first(me, N):
    if N != 32:
        return [lax.rem(me + k, N) for k in range(1, N)]
    core, x, y = lax.rem(me, 2), lax.rem(me // 2, 4), me // 8
    cores = [core, 1 - core]
    xs = [lax.rem(x + d, 4) * 2 for d in range(4)]
    ys = [lax.rem(y + d, 4) * 8 for d in range(4)]
    away = (0, 1, 2, 1)
    steps = [(dy, dx, dc) for dy in range(4) for dx in range(4) for dc in range(2)][1:]
    steps.sort(key=lambda s: -(away[s[0]] + away[s[1]]))
    return [ys[dy] + xs[dx] + cores[dc] for dy, dx, dc in steps]


def kernel(
    S, N,
    feats, ids, klist, kcount, g1, g2, wq_h, wk_h, wv_h, wo_h, wu_h, wd_h,
    out,
    wq, wk, wv, wo, wu, wd,
    oh, frecv, xbuf, xsend, gsend, halo, hn, qs, kx, vx, bias, tops, own, sbuf, pbuf, att, after_buf, hidden, fint, finrecv,
    wsem, fs_sem, fr_sem, hs_sem, hr_sem, as_sem, ar_sem, ns_sem, nr_sem,
):
    sec = lax.axis_index("section")
    me = lax.axis_index("dom")
    cols, rows = feats.shape[1], feats.shape[2]
    width = cols * S
    cw = width // CHUNKS
    halo_rows = N * PEER
    ext = rows + halo_rows
    pairs = HEADS // 2
    blocks = rows // BLOCK
    own_blocks = blocks
    all_blocks = ext // BLOCK

    barrier = pltpu.get_barrier_semaphore()

    @pl.loop(1, S)
    def _(k):
        pl.semaphore_signal(barrier, inc=1, device_id={"section": lax.rem(sec + k, S)}, device_id_type=MESH)

    @pl.loop(1, N)
    def _(k):
        pl.semaphore_signal(barrier, inc=1, device_id={"dom": lax.rem(me + k, N)}, device_id_type=MESH)

    weights = [
        pltpu.make_async_copy(h.at[0], v, wsem.at[i])
        for i, (h, v) in enumerate(((wq_h, wq), (wk_h, wk), (wv_h, wv), (wo_h, wo), (wu_h, wu), (wd_h, wd)))
    ]
    for w in weights:
        w.start()

    def feature_copy(m, source):
        return pltpu.make_async_remote_copy(
            src_ref=feats.at[m], dst_ref=frecv.at[m, pl.ds(source * cols, cols)],
            send_sem=fs_sem.at[m], recv_sem=fr_sem.at[m, source],
            device_id={"section": 0}, device_id_type=MESH,
        )

    spread = (
        lax.broadcasted_iota(jnp.int32, (halo_rows, N), 0) // PEER
        == lax.broadcasted_iota(jnp.int32, (halo_rows, N), 1)
    ).astype(BF16)
    of_peer = mm_t(spread, ids[...].astype(F32).astype(BF16))
    picked = jnp.where(
        lax.broadcasted_iota(jnp.int32, (halo_rows, PEER), 0) % PEER
        == lax.broadcasted_iota(jnp.int32, (halo_rows, PEER), 1),
        of_peer,
        0.0,
    )
    id_column = jnp.sum(picked, axis=1, keepdims=True).astype(jnp.int32)
    oh[...] = (id_column == lax.broadcasted_iota(jnp.int32, (halo_rows, rows), 1)).astype(F32).astype(BF16)

    pl.semaphore_wait(barrier, N - 1 + S - 1)

    @pl.when(sec != 0)
    def _():
        for m in range(MB):
            feature_copy(m, sec).start()

    for b in range(blocks):
        for e in range(all_blocks):
            times = jnp.int32(1 if e == b else 0)
            for j in range(klist.shape[1]):
                hit = jnp.logical_and(klist[b, j] == e, kcount[b] >= j + 1)
                times = times + jnp.where(hit, 1, 0)
            value = jnp.float32(DEAD)
            for t in range(len(LOG2)):
                value = jnp.where(times == t + 1, jnp.float32(LOG2[t]), value)
            bias[b, :, e * BLOCK:(e + 1) * BLOCK] = jnp.full((8, BLOCK), value, F32)
    for j in range(pairs):
        vx[j, :, 128:] = jnp.ones((ext, 128), BF16)

    gain1 = g1[...].astype(F32)
    gain2 = g2[...].astype(F32)

    def peer_copy(m, c, target):
        return pltpu.make_async_remote_copy(
            src_ref=gsend.at[m, c, pl.ds(target * PEER, PEER)],
            dst_ref=halo.at[m, c, pl.ds(me * PEER, PEER)],
            send_sem=as_sem.at[m], recv_sem=ar_sem.at[m],
            device_id={"dom": target}, device_id_type=MESH,
        )

    def hop_copy(m, c, target):
        return pltpu.make_async_remote_copy(
            src_ref=xsend.at[m, c], dst_ref=xbuf.at[m, c],
            send_sem=hs_sem.at[m, c], recv_sem=hr_sem.at[m, c],
            device_id={"section": target}, device_id_type=MESH,
        )

    def final_copy(m, target):
        return pltpu.make_async_remote_copy(
            src_ref=fint.at[m, pl.ds(target * cols, cols)], dst_ref=finrecv.at[m],
            send_sem=ns_sem.at[m, target], recv_sem=nr_sem.at[m],
            device_id={"section": target}, device_id_type=MESH,
        )

    qscale = (1.0 / float(width // HEADS) ** 0.5) * math.log2(math.e)
    mine = pl.ds(pl.multiple_of(me * PEER, PEER), PEER)
    partners = far_first(me, N)
    TILE = 64

    def exchange(m):
        @pl.when(sec == 0)
        def _():
            frecv[m, :cols, :] = feats[m]

        for c in range(CHUNKS):
            @pl.when(sec == 0)
            def _():
                for t in range(max(1, pl.cdiv(c * cw, cols)), pl.cdiv((c + 1) * cw, cols)):
                    feature_copy(m, t).wait_recv()
                xbuf[m, c] = frecv[m, c * cw:(c + 1) * cw, :].T

            @pl.when(sec != 0)
            def _():
                hop_copy(m, c, sec).wait_recv()

            gsend[m, c] = mm(oh[...], xbuf[m, c]).astype(BF16)

            for target in partners:
                peer_copy(m, c, target).start()

            halo[m, c, mine, :] = gsend[m, c, mine, :]

    def softmax_tile(scores, top):
        return jnp.concatenate(
            [jnp.exp2(scores[:, k:k + 128] - top) for k in range(0, scores.shape[1], 128)], axis=1
        ).astype(BF16)

    def tile_top(scores):
        best = scores[:, :128]
        for k in range(128, scores.shape[1], 128):
            best = jnp.maximum(best, scores[:, k:k + 128])
        return jnp.max(best, axis=1, keepdims=True)

    def scores_of(j, first, last):
        s = mm_t(qs[j], kx[j, first:last, :])
        for r in range(0, 2 * rows, BLOCK):
            b = (r // BLOCK) % blocks
            sbuf[j, r:r + BLOCK, :last - first] = s[r:r + BLOCK] + bias[b, 0:1, first:last]

    def own_part(m):
        x = jnp.concatenate([xbuf[m, c] for c in range(CHUNKS)], axis=1).astype(F32)
        normed = layer_norm(x, gain1)
        queries = (mm(normed, wq[...]) * qscale).astype(BF16)
        lane = lax.broadcasted_iota(jnp.int32, (rows, 128), 1)
        for j in range(pairs):
            qp = queries[:, j * 128:(j + 1) * 128]
            qs[j, :rows, :] = jnp.where(lane < 64, qp, jnp.zeros_like(qp))
            qs[j, rows:, :] = jnp.where(lane < 64, jnp.zeros_like(qp), qp)
        keys = mm(normed, wk[...]).astype(BF16)
        values = mm(normed, wv[...]).astype(BF16)
        for j in range(pairs):
            kx[j, :rows, :] = keys[:, j * 128:(j + 1) * 128]
            vx[j, :rows, :128] = values[:, j * 128:(j + 1) * 128]

        def middle(j):
            for r in range(0, 2 * rows, TILE):
                s = sbuf[j, r:r + TILE, :rows]
                top = jnp.broadcast_to(tile_top(s), (TILE, 128))
                tops[j, r:r + TILE, :] = top
                pbuf[j, r:r + TILE, :rows] = softmax_tile(s, top)

        scores_of(0, 0, rows)
        for j in range(pairs):
            if j + 1 < pairs:
                scores_of(j + 1, 0, rows)
            middle(j)
            own[j] = mm(pbuf[j, :, :rows], vx[j, :rows, :])

    def rest(m):
        arrived = halo.at[m, :, pl.ds(0, halo_rows - PEER)]
        pltpu.make_async_copy(arrived, arrived, ar_sem.at[m]).wait()
        for r in range(0, halo_rows, TILE):
            raw = jnp.concatenate([halo[m, c, r:r + TILE, :] for c in range(CHUNKS)], axis=1).astype(F32)
            hn[r:r + TILE, :] = layer_norm(raw, gain1)
        halo_keys = mm(hn[...], wk[...]).astype(BF16)
        for j in range(pairs):
            kx[j, rows:, :] = halo_keys[:, j * 128:(j + 1) * 128]
        halo_values = mm(hn[...], wv[...]).astype(BF16)
        for j in range(pairs):
            vx[j, rows:, :128] = halo_values[:, j * 128:(j + 1) * 128]

        def middle(j):
            for r in range(0, 2 * rows, TILE):
                s = sbuf[j, r:r + TILE, :halo_rows]
                before = tops[j, r:r + TILE, :]
                top = jnp.maximum(before, tile_top(s))
                pbuf[j, r:r + TILE, :halo_rows] = softmax_tile(s, top)
                shrink = jnp.exp2(before - top)
                own[j, r:r + TILE, :] = own[j, r:r + TILE, :] * jnp.concatenate([shrink, shrink], axis=1)

        lane = lax.broadcasted_iota(jnp.int32, (rows, 128), 1)

        def mix(j):
            o = mm(pbuf[j, :, :halo_rows], vx[j, rows:, :]) + own[j]
            top_part = jnp.where(lane < 64, o[:rows, :128], o[rows:, :128])
            weight = jnp.where(lane < 64, o[:rows, 128:], o[rows:, 128:])
            att[:, j * 128:(j + 1) * 128] = (top_part / weight).astype(BF16)

        scores_of(0, rows, ext)
        for j in range(pairs):
            if j + 1 < pairs:
                scores_of(j + 1, rows, ext)
            middle(j)
            mix(j)

        x = jnp.concatenate([xbuf[m, c] for c in range(CHUNKS)], axis=1).astype(F32)
        after = x + mm(att[...], wo[...])
        after_buf[...] = after
        normed_two = layer_norm(after, gain2)
        ff = wu.shape[1]
        for k in range(0, ff, 256):
            up = mm(normed_two, wu[:, k:k + 256])
            hidden[:, k:k + 256] = (0.5 * up * (1.0 + lax.erf(up * (0.5 ** 0.5)))).astype(BF16)
        step = max(cw, 256)
        for k in range(0, width, step):
            part = (after_buf[:, k:k + step] + mm(hidden[...], wd[:, k:k + step])).astype(BF16)
            for c in range(k // cw, (k + step) // cw):
                xsend[m, c] = part[:, c * cw - k:(c + 1) * cw - k]

            @pl.when(sec != S - 1)
            def _():
                for c in range(k // cw, (k + step) // cw):
                    hop_copy(m, c, sec + 1).start()

        @pl.when(sec == S - 1)
        def _():
            for c in range(CHUNKS):
                fint[m, c * cw:(c + 1) * cw, :] = xsend[m, c].T
            finrecv[m] = fint[m, (S - 1) * cols:, :]
            for t in sorted(range(S - 1), key=lambda t: -min(S - 1 - t, t + 1)):
                final_copy(m, t).start()

    exchange(0)
    for w in weights[:3]:
        w.wait()
    own_part(0)
    exchange(1)
    for w in weights[3:]:
        w.wait()
    rest(0)
    own_part(1)
    rest(1)

    for m in range(MB):
        @pl.when(sec != S - 1)
        def _():
            final_copy(m, sec).wait_recv()

        out[m] = finrecv[m].astype(F32)

    for m in range(MB):
        @pl.when(sec != 0)
        def _():
            feature_copy(m, sec).wait_send()

        @pl.when(sec != S - 1)
        def _():
            for c in range(CHUNKS):
                hop_copy(m, c, sec + 1).wait_send()

        @pl.when(sec == S - 1)
        def _():
            for t in range(S - 1):
                final_copy(m, t).wait_send()

        left = gsend.at[m, :, pl.ds(0, halo_rows - PEER)]
        pltpu.make_async_copy(left, left, as_sem.at[m]).wait()


def on_device(S, N, feats, ids, klist, kcount, g1, wq, wk, wv, wo, g2, wu, wd):
    mb, rows, cols = feats.shape
    width = cols * S
    ff = wu.shape[2]
    halo_rows = N * PEER
    ext = rows + halo_rows
    pairs = HEADS // 2
    cw = width // CHUNKS
    vmem = pl.BlockSpec(memory_space=pltpu.VMEM)
    smem = pl.BlockSpec(memory_space=pltpu.SMEM)
    hbm = pl.BlockSpec(memory_space=pl.ANY)
    dma = pltpu.SemaphoreType.DMA
    result = pl.pallas_call(
        functools.partial(kernel, S, N),
        out_shape=jax.ShapeDtypeStruct((mb, cols, rows), F32),
        in_specs=[vmem, vmem, smem, smem, vmem, vmem] + [hbm] * 6,
        out_specs=vmem,
        scratch_shapes=[
            pltpu.VMEM((width, width), BF16),
            pltpu.VMEM((width, width), BF16),
            pltpu.VMEM((width, width), BF16),
            pltpu.VMEM((width, width), BF16),
            pltpu.VMEM((width, ff), BF16),
            pltpu.VMEM((ff, width), BF16),
            pltpu.VMEM((halo_rows, rows), BF16),
            pltpu.VMEM((mb, width, rows), BF16),
            pltpu.VMEM((mb, CHUNKS, rows, cw), BF16),
            pltpu.VMEM((mb, CHUNKS, rows, cw), BF16),
            pltpu.VMEM((mb, CHUNKS, halo_rows, cw), BF16),
            pltpu.VMEM((mb, CHUNKS, halo_rows, cw), BF16),
            pltpu.VMEM((halo_rows, width), BF16),
            pltpu.VMEM((pairs, 2 * rows, 128), BF16),
            pltpu.VMEM((pairs, ext, 128), BF16),
            pltpu.VMEM((pairs, ext, 256), BF16),
            pltpu.VMEM((rows // BLOCK, 8, ext), F32),
            pltpu.VMEM((pairs, 2 * rows, 128), F32),
            pltpu.VMEM((pairs, 2 * rows, 256), F32),
            pltpu.VMEM((pairs, 2 * rows, max(halo_rows, rows)), F32),
            pltpu.VMEM((pairs, 2 * rows, max(halo_rows, rows)), BF16),
            pltpu.VMEM((rows, width), BF16),
            pltpu.VMEM((rows, width), F32),
            pltpu.VMEM((rows, ff), BF16),
            pltpu.VMEM((mb, width, rows), BF16),
            pltpu.VMEM((mb, cols, rows), BF16),
            dma((6,)),
            dma((mb,)),
            dma((mb, S)),
            dma((mb, CHUNKS)),
            dma((mb, CHUNKS)),
            dma((mb,)),
            dma((mb,)),
            dma((mb, S)),
            dma((mb,)),
        ],
        compiler_params=pltpu.CompilerParams(collective_id=0, has_side_effects=True),
    )(jnp.swapaxes(feats, 1, 2), ids.T, klist, kcount, g1, g2, wq, wk, wv, wo, wu, wd)
    return jnp.swapaxes(result, 1, 2)


def solution(mesh):
    return jax.shard_map(
        functools.partial(on_device, mesh.shape["section"], mesh.shape["dom"]),
        mesh=mesh,
        in_specs=(
            P(None, "dom", "section"),
            P("dom", None),
            P("dom", None),
            P("dom"),
            P("section", None),
            P("section", None, None),
            P("section", None, None),
            P("section", None, None),
            P("section", None, None),
            P("section", None),
            P("section", None, None),
            P("section", None, None),
        ),
        out_specs=P(None, "dom", "section"),
        check_vma=False,
    )
```
